32 devices in a mesh: seq: 16 (over z, x, core), head: 2 (over y).
Axes of the slice: x: 2, y: 2, z: 4, core: 2. Of those that a mesh axis runs over, the one named last changes fastest.
Arguments:
- queries: bfloat16 [4096, 4096], P('seq', 'head'), may hold values from -8 to 8
- keys: bfloat16 [4096, 4096], P('seq', 'head'), may hold values from -8 to 8
- values: bfloat16 [4096, 4096], P('seq', 'head'), may hold values from -6 to 6
- features: float32 [32, 128, 256], P('head'), may hold values from -6 to 6
- output_proj_weight: bfloat16 [4096, 4096], P('head', 'seq'), may hold values from -0.125 to 0.125
Outputs:
- mixed: bfloat16 [4096, 4096], P('seq', 'head')
The draws below stay inside these ranges and needn't reach their ends.
All inputs are finite; a program needn't handle non-finite values.
Results may differ from the reference program's by a relative error of at most 0.005.
Values may be sent and summed in bfloat16 or wider, within the bound.
A program may use at most 192 MiB of HBM per device.

```python
import math
import jax
import jax.numpy as jnp
from jax import lax

D = 4096
HEADS = 32
DH = 128
M = 256
TOKENS = 4096


def spiked(values, own_key, source, target, blocks, factor):
    owner, partner = [(jnp.arange(values.shape[axis_at]) // (values.shape[axis_at] // blocks)).reshape([-1 if axis == axis_at else 1 for axis in range(values.ndim)]) for axis_at in (source, target)]
    chosen = jax.random.permutation(own_key, blocks)[partner]
    strong = (owner == chosen) | (owner == (partner + blocks // 2) % blocks)
    return jnp.where(strong, factor * values, values)


def levels(stream_key, extent, split, low, high):
    loudness = 1.0
    for position, shards_of in split:
        draws = jax.random.uniform(jax.random.fold_in(jax.random.fold_in(stream_key, 6), position), (shards_of,), jnp.float32, low / len(split), high / len(split))
        loudness = loudness * jnp.repeat(jnp.exp(draws), extent[position] // shards_of).reshape((-1,) + (1,) * (len(extent) - 1 - position))
    return loudness


def noise(own_key, extent, spread, most, split=(), kind=jnp.bfloat16):
    level = levels(own_key, extent, split, -0.22, 0.18) if split else 1.0
    values = jax.random.normal(own_key, extent, jnp.float32) * spread * level
    return jnp.minimum(jnp.maximum(values, -most), most).astype(kind)


def heavy_noise(own_key, dims, scale, reach, split, heavy, held_as=jnp.bfloat16):
    values = scale * jax.random.normal(own_key, dims, jnp.float32)
    if split:
        values = values * levels(own_key, dims, split, -0.22, 0.18)
    return jnp.clip(spiked(values, jax.random.fold_in(own_key, 3), *heavy), -reach, reach).astype(held_as)


def setup_inputs(seed: int = 0) -> dict:
    splits = jax.random.split(jax.random.key(seed), 6)
    return {
        "queries": noise(splits[0], (TOKENS, HEADS * DH), 1.25, 8.0, ((0, 16), (1, 2))),
        "keys": noise(splits[1], (TOKENS, HEADS * DH), 1.25, 8.0, ((0, 16), (1, 2))),
        "values": noise(splits[2], (TOKENS, HEADS * DH), 1.0, 6.0, ((0, 16), (1, 2))),
        "features": noise(splits[3], (HEADS, DH, M), 1.0, 6.0, ((0, 2),), jnp.float32),
        "output_proj_weight": heavy_noise(splits[4], (HEADS * DH, D), (HEADS * DH) ** -0.5, 0.125, ((0, 2), (1, 16)), (0, 1, 16, 2.0)),
    }


def feature_map(x, direction):
    x = x * DH ** (-0.25)
    proj = jnp.dot(x, direction, precision=lax.Precision.HIGHEST)
    return jnp.exp(proj - 0.5 * lax.optimization_barrier(jnp.sum(x * x, axis=-1, keepdims=True))) / math.sqrt(M)

def head_attend(inputs):
    query, key, value, direction = inputs
    block = math.gcd(TOKENS, 512)
    count = TOKENS // block
    query = query.reshape(count, block, DH)
    key = key.reshape(count, block, DH)
    value = value.reshape(count, block, DH)
    lower = jnp.tril(jnp.ones((block, block), jnp.float32))

    def step(carry, piece):
        state, total = carry
        q_block, k_block, v_block = piece
        query_random_feats = feature_map(q_block, direction)
        key_random_feats = feature_map(k_block, direction)
        causal_scores = jnp.dot(query_random_feats, key_random_feats.T, precision=lax.Precision.HIGHEST) * lower
        numer = jnp.dot(causal_scores, v_block, precision=lax.Precision.HIGHEST) + jnp.dot(query_random_feats, state, precision=lax.Precision.HIGHEST)
        denom = lax.optimization_barrier(jnp.sum(causal_scores, axis=1)) + jnp.dot(query_random_feats, total, precision=lax.Precision.HIGHEST)
        state = state + jnp.dot(key_random_feats.T, v_block, precision=lax.Precision.HIGHEST)
        total = total + lax.optimization_barrier(jnp.sum(key_random_feats, axis=0))
        return ((state, total), numer / denom[:, None])
    init = (jnp.zeros((M, DH), jnp.float32), jnp.zeros((M,), jnp.float32))
    _, final_output = lax.scan(step, init, (query, key, value))
    return final_output.reshape(TOKENS, DH)

def reference(queries, keys, values, features, output_proj_weight):

    def split_heads(arr):
        return arr.astype(jnp.float32).reshape(TOKENS, HEADS, DH).transpose(1, 0, 2)
    final_output = lax.map(head_attend, (split_heads(queries), split_heads(keys), split_heads(values), features))
    attended = final_output.transpose(1, 0, 2).reshape(TOKENS, HEADS * DH).astype(jnp.bfloat16)
    return jnp.dot(attended, output_proj_weight, preferred_element_type=jnp.float32).astype(jnp.bfloat16)
```

```python
import math

import jax
import jax.numpy as jnp
from jax import lax
from jax.sharding import PartitionSpec as P

DH = 128
M = 256
HIGH = lax.Precision.HIGHEST


def feature_map(x, direction):
    x = x * DH ** (-0.25)
    proj = jnp.einsum("htd,hdm->htm", x, direction, precision=HIGH)
    return jnp.exp(proj - 0.5 * jnp.sum(x * x, axis=-1, keepdims=True)) / math.sqrt(M)


def shards(queries, keys, values, features, output_proj_weight):
    tok_rows = queries.shape[0]
    local_heads = features.shape[0]
    devices, here = lax.axis_size("seq"), lax.axis_index("seq")
    halves, half = lax.axis_size("head"), lax.axis_index("head")

    def split_heads(arr):
        return arr.astype(jnp.float32).reshape(tok_rows, local_heads, DH).transpose(1, 0, 2)

    kf = feature_map(split_heads(keys), features)
    v = split_heads(values)
    v = jnp.concatenate([v, jnp.ones((local_heads, tok_rows, 8), jnp.float32)], axis=2)
    state = jnp.einsum("htp,htk->hpk", v, kf, precision=HIGH)
    states = lax.all_gather(state.astype(jnp.bfloat16), "seq")
    state, weight = lax.optimization_barrier((state, output_proj_weight))
    whole = lax.all_gather(weight, "seq", axis=1, tiled=True)
    qf = feature_map(split_heads(queries), features)
    lower = jnp.tril(jnp.ones((tok_rows, tok_rows), jnp.float32))
    scores = jnp.einsum("htm,hsm->hts", qf, kf, precision=HIGH) * lower
    both = jnp.einsum("hts,hsd->htd", scores, v, precision=HIGH)
    earlier = (jnp.arange(devices) < here)[:, None, None, None]
    prior = jnp.sum(jnp.where(earlier, states.astype(jnp.float32), 0.0), axis=0)
    both = both + jnp.einsum("htk,hpk->htp", qf, prior, precision=HIGH)
    attended = both[:, :, :DH] / both[:, :, DH : DH + 1]
    attended = attended.transpose(1, 0, 2).reshape(tok_rows, local_heads * DH).astype(jnp.bfloat16)
    partial = jnp.dot(attended, whole, preferred_element_type=jnp.float32)
    width = partial.shape[1] // halves
    total = lax.dynamic_slice_in_dim(partial, half * width, width, 1)
    for shift in range(1, halves):
        theirs = lax.rem(half + shift, halves)
        piece = lax.dynamic_slice_in_dim(partial, theirs * width, width, 1).astype(jnp.bfloat16)
        got = lax.ppermute(piece, "head", [(i, (i + shift) % halves) for i in range(halves)])
        total = total + got.astype(jnp.float32)
    return total.astype(jnp.bfloat16)


def solution(mesh):
    in_specs = (
        P("seq", "head"),
        P("seq", "head"),
        P("seq", "head"),
        P("head", None, None),
        P("head", "seq"),
    )
    return jax.shard_map(
        shards, mesh=mesh, in_specs=in_specs, out_specs=P("seq", "head"), check_vma=False
    )
```

```python
import functools
import math

import jax
import jax.numpy as jnp
from jax import lax
from jax.experimental import pallas as pl
from jax.experimental.pallas import tpu as pltpu
from jax.sharding import PartitionSpec as P

DH = 128
M = 256
HIGH = lax.Precision.HIGHEST


def feature_map(x, direction):
    x = x * DH ** (-0.25)
    proj = jnp.einsum("htd,hdm->htm", x, direction, precision=HIGH)
    return jnp.exp(proj - 0.5 * jnp.sum(x * x, axis=-1, keepdims=True)) / math.sqrt(M)


def plain(queries, keys, values, features, output_proj_weight):
    tok_rows = queries.shape[0]
    local_heads = features.shape[0]
    devices, here = lax.axis_size("seq"), lax.axis_index("seq")
    halves, half = lax.axis_size("head"), lax.axis_index("head")

    def split_heads(arr):
        return arr.astype(jnp.float32).reshape(tok_rows, local_heads, DH).transpose(1, 0, 2)

    kf = feature_map(split_heads(keys), features)
    v = split_heads(values)
    v = jnp.concatenate([v, jnp.ones((local_heads, tok_rows, 8), jnp.float32)], axis=2)
    state = jnp.einsum("htp,htk->hpk", v, kf, precision=HIGH)
    states = lax.all_gather(state.astype(jnp.bfloat16), "seq")
    state, weight = lax.optimization_barrier((state, output_proj_weight))
    whole = lax.all_gather(weight, "seq", axis=1, tiled=True)
    qf = feature_map(split_heads(queries), features)
    lower = jnp.tril(jnp.ones((tok_rows, tok_rows), jnp.float32))
    scores = jnp.einsum("htm,hsm->hts", qf, kf, precision=HIGH) * lower
    both = jnp.einsum("hts,hsd->htd", scores, v, precision=HIGH)
    earlier = (jnp.arange(devices) < here)[:, None, None, None]
    prior = jnp.sum(jnp.where(earlier, states.astype(jnp.float32), 0.0), axis=0)
    both = both + jnp.einsum("htk,hpk->htp", qf, prior, precision=HIGH)
    attended = both[:, :, :DH] / both[:, :, DH : DH + 1]
    attended = attended.transpose(1, 0, 2).reshape(tok_rows, local_heads * DH).astype(jnp.bfloat16)
    partial = jnp.dot(attended, whole, preferred_element_type=jnp.float32)
    width = partial.shape[1] // halves
    total = lax.dynamic_slice_in_dim(partial, half * width, width, 1)
    for shift in range(1, halves):
        theirs = lax.rem(half + shift, halves)
        piece = lax.dynamic_slice_in_dim(partial, theirs * width, width, 1).astype(jnp.bfloat16)
        got = lax.ppermute(piece, "head", [(i, (i + shift) % halves) for i in range(halves)])
        total = total + got.astype(jnp.float32)
    return total.astype(jnp.bfloat16)


ROWS = DH + 8
PLANE, DEPTH = 4, 4
GROUPS = 4


def kernel_body(heads, q_ref, k_ref, v_ref, f_ref, w_hbm, out_ref, wbuf, kf, qf, vt, both, state,
                sib_state, below, xsend, xrecv, prior, back, att, acc, psend, precv,
                load_sem, w_send, w_recv, s_send, s_recv, z_send, z_recv, x_send, x_recv,
                b_send, b_recv, p_send, p_recv):
    tok = q_ref.shape[0]
    half_heads = heads // 2
    per = half_heads // GROUPS
    me, y = lax.axis_index("seq"), lax.axis_index("head")
    n = lax.axis_size("seq")
    z, x, c = me // PLANE, (me // 2) % 2, me % 2
    sib, xn, up, down = me + 1 - 2 * c, me + 2 - 4 * x, me + PLANE, me - PLANE
    has_up, has_down = z < DEPTH - 1, z > 0

    load = pltpu.make_async_copy(w_hbm, wbuf.at[me], load_sem)
    load.start()
    barrier = pltpu.get_barrier_semaphore()

    def greet(device):
        pl.semaphore_signal(barrier, inc=1, device_id=device, device_id_type=pl.DeviceIdType.MESH)

    greet((sib, y))
    greet((xn, y))
    greet((me, 1 - y))

    @pl.when(has_up)
    def _():
        greet((up, y))

    @pl.when(has_down)
    def _():
        greet((down, y))

    pl.semaphore_wait(barrier, 3 + has_up.astype(jnp.int32) + has_down.astype(jnp.int32))

    def remote(src, dst, ssem, rsem, device):
        return pltpu.make_async_remote_copy(
            src_ref=src, dst_ref=dst, send_sem=ssem, recv_sem=rsem, device_id=device,
            device_id_type=pl.DeviceIdType.MESH)

    started = []

    def go(cond, copy):
        if cond is None:
            copy.start()
        else:
            pl.when(cond)(copy.start)
        started.append((cond, copy))

    def block(slot, way, device):
        return remote(wbuf.at[slot], wbuf.at[slot], w_send.at[slot, way], w_recv.at[slot],
                      (device, y))

    def arrived(slot):
        block(slot, 3, sib).wait_recv()

    load.wait()
    go(has_up, block(me, 0, up))
    go(has_down, block(me, 1, down))
    go(None, block(me, 2, xn))
    go(None, block(me, 3, sib))

    def both_ways(cond, *copies):
        for one in copies:
            go(cond, one)

    def along(d):
        above, under = me + PLANE * d, me - PLANE * d
        ok = z >= d

        @pl.when(ok)
        def _():
            arrived(under)
        go(jnp.logical_and(ok, has_up), block(under, 0, up))
        both_ways(ok, block(under, 2, xn), block(under, 3, sib))
        ok = z + d < DEPTH

        @pl.when(ok)
        def _():
            arrived(above)
        go(jnp.logical_and(ok, has_down), block(above, 1, down))
        both_ways(ok, block(above, 2, xn), block(above, 3, sib))

    def across(d):
        if d == 0:
            arrived(xn)
            go(None, block(xn, 3, sib))
            return
        for slot, ok in ((xn - PLANE * d, z >= d), (xn + PLANE * d, z + d < DEPTH)):
            pl.when(ok)(functools.partial(arrived, slot))
            go(ok, block(slot, 3, sib))

    def head_cols(h):
        return pl.ds(pl.multiple_of(h * DH, DH), DH)

    def feature_map(ref, h):
        t = ref[:, head_cols(h)].astype(jnp.float32) * DH ** (-0.25)
        proj = jnp.dot(t, f_ref[h], precision=HIGH, preferred_element_type=jnp.float32)
        return jnp.exp(proj - 0.5 * jnp.sum(t * t, axis=-1, keepdims=True)) * (1 / math.sqrt(M))

    @pl.loop(0, heads)
    def _(h):
        kf[h] = feature_map(k_ref, h)
        vt[h, :DH, :] = v_ref[:, head_cols(h)].astype(jnp.float32).T
        vt[h, DH:, :] = jnp.ones((ROWS - DH, tok), jnp.float32)
        state[h] = jnp.dot(vt[h], kf[h], precision=HIGH, preferred_element_type=jnp.float32)

    mine, other = c * half_heads, (1 - c) * half_heads
    swap = remote(state.at[pl.ds(other, half_heads)], sib_state, s_send, s_recv, (sib, y))
    go(None, swap)
    swap.wait_recv()

    lower = (lax.broadcasted_iota(jnp.int32, (tok, tok), 1)
             <= lax.broadcasted_iota(jnp.int32, (tok, tok), 0))

    def transposed(a, b):
        return lax.dot_general(a, b, (((1,), (1,)), ((), ())), precision=HIGH,
                               preferred_element_type=jnp.float32)

    def local_heads(start, count):
        @pl.loop(start, start + count)
        def _(h):
            qf[h] = feature_map(q_ref, h)
            scores = jnp.where(lower, transposed(qf[h], kf[h]), 0.0)
            both[h] = transposed(scores, vt[h])

    at_x0 = (x == 0).astype(jnp.float32)
    for g in range(GROUPS):
        part = pl.ds(g * per, per)
        hop = remote(back.at[part], below.at[part], z_send.at[g], z_recv.at[g], (up, y))

        @pl.when(has_down)
        def _():
            hop.wait_recv()

        @pl.when(z == 0)
        def _():
            below[part] = jnp.zeros((per, ROWS, M), jnp.float32)

        chip = state[pl.ds(mine + g * per, per)] + sib_state[part]
        back[part] = below[part] + chip
        xsend[part] = below[part] + at_x0 * chip
        go(has_up, hop)
        go(None, remote(xsend.at[part], xrecv.at[part], x_send.at[g], x_recv.at[g], (xn, y)))
        local_heads(g * (heads // GROUPS), heads // GROUPS)
        if g == 1:
            along(1)
            across(0)

    at_c0, at_c1 = (c == 0).astype(jnp.float32), (c == 1).astype(jnp.float32)
    for g in range(GROUPS):
        part = pl.ds(g * per, per)
        own = pl.ds(mine + g * per, per)
        remote(xsend.at[part], xrecv.at[part], x_send.at[g], x_recv.at[g], (xn, y)).wait_recv()
        base = below[part] + xrecv[part]
        xrecv[part] = base + at_c0 * state[own]
        prior[own] = base + at_c1 * sib_state[part]
        go(None, remote(xrecv.at[part], prior.at[own], b_send.at[g], b_recv.at[g], (sib, y)))

    def finish(start):
        @pl.loop(0, half_heads)
        def _(i):
            h = start + i
            total = both[h] + transposed(qf[h], prior[h])
            att[:, head_cols(h)] = (total[:, :DH] / total[:, DH : DH + 1]).astype(att.dtype)

    finish(mine)
    along(2)
    across(1)
    for g in range(GROUPS):
        theirs = pl.ds(other + g * per, per)
        remote(xrecv.at[pl.ds(g * per, per)], prior.at[theirs], b_send.at[g], b_recv.at[g],
               (sib, y)).wait_recv()
    finish(other)

    width = wbuf.shape[2]
    halfn = n // 2

    def out_copy(b):
        i = b % halfn
        return remote(psend.at[i], precv.at[i], p_send.at[i], p_recv.at[i], (me, 1 - y))

    def bit(a, b):
        return (a + b) % 2

    def project(first, count):
        @pl.loop(first, first + count)
        def _(i):
            b = ((bit(z // 2, i // 8) * 2 + bit(z % 2, (i // 4) % 2)) * PLANE
                 + bit(x, (i // 2) % 2) * 2 + bit(c, i % 2))

            @pl.when(i % 2 == 1)
            def _():
                arrived(b)
            piece = jnp.dot(att[...], wbuf[b], preferred_element_type=jnp.float32)

            @pl.when(b // halfn == y)
            def _():
                acc[b % halfn] = piece

            @pl.when(b // halfn != y)
            def _():
                psend[b % halfn] = piece.astype(psend.dtype)
                out_copy(b).start()

    project(0, 2 * PLANE)
    along(3)
    across(2)
    project(2 * PLANE, PLANE)
    across(3)
    project(3 * PLANE, PLANE)
    for i in range(halfn):
        out_copy(i).wait_recv()
        out_ref[:, i * width : (i + 1) * width] = (
            acc[i] + precv[i].astype(jnp.float32)).astype(out_ref.dtype)
    for i in range(halfn):
        out_copy(i).wait_send()
    for cond, copy in started:
        if cond is None:
            copy.wait_send()
        else:
            pl.when(cond)(copy.wait_send)


def fused(queries, keys, values, features, weight):
    tok, columns = queries.shape
    heads = features.shape[0]
    n = lax.axis_size("seq")
    depth, width = weight.shape
    half = heads // 2
    f32, bf16 = jnp.float32, jnp.bfloat16
    vmem = pltpu.VMEM
    dma = pltpu.SemaphoreType.DMA
    inner = [pl.BlockSpec(memory_space=pltpu.VMEM)] * 4
    return pl.pallas_call(
        functools.partial(kernel_body, heads),
        out_shape=jax.ShapeDtypeStruct((tok, width * n // 2), bf16),
        in_specs=inner + [pl.BlockSpec(memory_space=pl.ANY)],
        out_specs=pl.BlockSpec(memory_space=pltpu.VMEM),
        scratch_shapes=[
            vmem((n, depth, width), bf16),
            vmem((heads, tok, M), f32),
            vmem((heads, tok, M), f32),
            vmem((heads, ROWS, tok), f32),
            vmem((heads, tok, ROWS), f32),
            vmem((heads, ROWS, M), f32),
            vmem((half, ROWS, M), f32),
            vmem((half, ROWS, M), f32),
            vmem((half, ROWS, M), f32),
            vmem((half, ROWS, M), f32),
            vmem((heads, ROWS, M), f32),
            vmem((half, ROWS, M), f32),
            vmem((tok, columns), bf16),
            vmem((n // 2, tok, width), f32),
            vmem((n // 2, tok, width), bf16),
            vmem((n // 2, tok, width), bf16),
            dma, dma((n, 4)), dma((n,)), dma, dma,
            dma((GROUPS,)), dma((GROUPS,)), dma((GROUPS,)), dma((GROUPS,)),
            dma((GROUPS,)), dma((GROUPS,)), dma((n // 2,)), dma((n // 2,)),
        ],
        compiler_params=pltpu.CompilerParams(
            collective_id=0, has_side_effects=True, vmem_limit_bytes=63 << 20),
    )(queries, keys, values, features, weight)


def shards(queries, keys, values, features, output_proj_weight):
    fits = (
        lax.axis_size("seq") == PLANE * DEPTH
        and lax.axis_size("head") == 2
        and features.shape[0] % (2 * GROUPS) == 0
        and output_proj_weight.shape[1] % 128 == 0
    )
    step = fused if fits else plain
    return step(queries, keys, values, features, output_proj_weight)


def solution(mesh):
    in_specs = (
        P("seq", "head"),
        P("seq", "head"),
        P("seq", "head"),
        P("head", None, None),
        P("head", "seq"),
    )
    return jax.shard_map(
        shards, mesh=mesh, in_specs=in_specs, out_specs=P("seq", "head"), check_vma=False
    )
```

```python
import functools
import math

import jax
import jax.numpy as jnp
from jax import lax
from jax.experimental import pallas as pl
from jax.experimental.pallas import tpu as pltpu
from jax.sharding import PartitionSpec as P

DH = 128
M = 256
HIGH = lax.Precision.HIGHEST


def feature_map(x, direction):
    x = x * DH ** (-0.25)
    proj = jnp.einsum("htd,hdm->htm", x, direction, precision=HIGH)
    return jnp.exp(proj - 0.5 * jnp.sum(x * x, axis=-1, keepdims=True)) / math.sqrt(M)


def plain(queries, keys, values, features, output_proj_weight):
    tok_rows = queries.shape[0]
    local_heads = features.shape[0]
    devices, here = lax.axis_size("seq"), lax.axis_index("seq")
    halves, half = lax.axis_size("head"), lax.axis_index("head")

    def split_heads(arr):
        return arr.astype(jnp.float32).reshape(tok_rows, local_heads, DH).transpose(1, 0, 2)

    kf = feature_map(split_heads(keys), features)
    v = split_heads(values)
    v = jnp.concatenate([v, jnp.ones((local_heads, tok_rows, 8), jnp.float32)], axis=2)
    state = jnp.einsum("htp,htk->hpk", v, kf, precision=HIGH)
    states = lax.all_gather(state.astype(jnp.bfloat16), "seq")
    state, weight = lax.optimization_barrier((state, output_proj_weight))
    whole = lax.all_gather(weight, "seq", axis=1, tiled=True)
    qf = feature_map(split_heads(queries), features)
    lower = jnp.tril(jnp.ones((tok_rows, tok_rows), jnp.float32))
    scores = jnp.einsum("htm,hsm->hts", qf, kf, precision=HIGH) * lower
    both = jnp.einsum("hts,hsd->htd", scores, v, precision=HIGH)
    earlier = (jnp.arange(devices) < here)[:, None, None, None]
    prior = jnp.sum(jnp.where(earlier, states.astype(jnp.float32), 0.0), axis=0)
    both = both + jnp.einsum("htk,hpk->htp", qf, prior, precision=HIGH)
    attended = both[:, :, :DH] / both[:, :, DH : DH + 1]
    attended = attended.transpose(1, 0, 2).reshape(tok_rows, local_heads * DH).astype(jnp.bfloat16)
    partial = jnp.dot(attended, whole, preferred_element_type=jnp.float32)
    width = partial.shape[1] // halves
    total = lax.dynamic_slice_in_dim(partial, half * width, width, 1)
    for shift in range(1, halves):
        theirs = lax.rem(half + shift, halves)
        piece = lax.dynamic_slice_in_dim(partial, theirs * width, width, 1).astype(jnp.bfloat16)
        got = lax.ppermute(piece, "head", [(i, (i + shift) % halves) for i in range(halves)])
        total = total + got.astype(jnp.float32)
    return total.astype(jnp.bfloat16)


ROWS = DH + 8
PLANE, DEPTH = 4, 4
GROUPS = 4


def kernel_body(heads, q_ref, k_ref, v_ref, f_ref, w_hbm, out_ref, wbuf, kf, qf, vt, both, state,
                sib_state, below, xsend, xrecv, prior, back, att, acc, psend, precv,
                load_sem, w_send, w_recv, s_send, s_recv, z_send, z_recv, x_send, x_recv,
                b_send, b_recv, p_send, p_recv):
    tok = q_ref.shape[0]
    half_heads = heads // 2
    per = half_heads // GROUPS
    me, y = lax.axis_index("seq"), lax.axis_index("head")
    n = lax.axis_size("seq")
    z, x, c = me // PLANE, (me // 2) % 2, me % 2
    sib, xn, up, down = me + 1 - 2 * c, me + 2 - 4 * x, me + PLANE, me - PLANE
    has_up, has_down = z < DEPTH - 1, z > 0

    load = pltpu.make_async_copy(w_hbm, wbuf.at[me], load_sem)
    load.start()
    barrier = pltpu.get_barrier_semaphore()

    def greet(device):
        pl.semaphore_signal(barrier, inc=1, device_id=device, device_id_type=pl.DeviceIdType.MESH)

    greet((sib, y))
    greet((xn, y))
    greet((me, 1 - y))

    @pl.when(has_up)
    def _():
        greet((up, y))

    @pl.when(has_down)
    def _():
        greet((down, y))

    pl.semaphore_wait(barrier, 3 + has_up.astype(jnp.int32) + has_down.astype(jnp.int32))

    def remote(src, dst, ssem, rsem, device):
        return pltpu.make_async_remote_copy(
            src_ref=src, dst_ref=dst, send_sem=ssem, recv_sem=rsem, device_id=device,
            device_id_type=pl.DeviceIdType.MESH)

    started = []

    def go(cond, copy):
        if cond is None:
            copy.start()
        else:
            pl.when(cond)(copy.start)
        started.append((cond, copy))

    def block(slot, way, device):
        return remote(wbuf.at[slot], wbuf.at[slot], w_send.at[slot, way], w_recv.at[slot],
                      (device, y))

    def arrived(slot):
        block(slot, 3, sib).wait_recv()

    load.wait()
    go(has_up, block(me, 0, up))
    go(has_down, block(me, 1, down))
    go(None, block(me, 2, xn))
    go(None, block(me, 3, sib))

    def both_ways(cond, *copies):
        for one in copies:
            go(cond, one)

    def along(d):
        above, under = me + PLANE * d, me - PLANE * d
        ok = z >= d

        @pl.when(ok)
        def _():
            arrived(under)
        go(jnp.logical_and(ok, has_up), block(under, 0, up))
        both_ways(ok, block(under, 2, xn), block(under, 3, sib))
        ok = z + d < DEPTH

        @pl.when(ok)
        def _():
            arrived(above)
        go(jnp.logical_and(ok, has_down), block(above, 1, down))
        both_ways(ok, block(above, 2, xn), block(above, 3, sib))

    def across(d):
        if d == 0:
            arrived(xn)
            go(None, block(xn, 3, sib))
            return
        for slot, ok in ((xn - PLANE * d, z >= d), (xn + PLANE * d, z + d < DEPTH)):
            pl.when(ok)(functools.partial(arrived, slot))
            go(ok, block(slot, 3, sib))

    def head_cols(h):
        return pl.ds(pl.multiple_of(h * DH, DH), DH)

    def feature_map(ref, h):
        t = ref[:, head_cols(h)].astype(jnp.float32) * DH ** (-0.25)
        proj = jnp.dot(t, f_ref[h], precision=HIGH, preferred_element_type=jnp.float32)
        return jnp.exp(proj - 0.5 * jnp.sum(t * t, axis=-1, keepdims=True)) * (1 / math.sqrt(M))

    @pl.loop(0, heads)
    def _(h):
        kf[h] = feature_map(k_ref, h)
        vt[h, :DH, :] = v_ref[:, head_cols(h)].astype(jnp.float32).T
        vt[h, DH:, :] = jnp.ones((ROWS - DH, tok), jnp.float32)
        state[h] = jnp.dot(vt[h], kf[h], precision=HIGH, preferred_element_type=jnp.float32)

    mine, other = c * half_heads, (1 - c) * half_heads
    swap = remote(state.at[pl.ds(other, half_heads)], sib_state, s_send, s_recv, (sib, y))
    go(None, swap)
    swap.wait_recv()

    lower = (lax.broadcasted_iota(jnp.int32, (tok, tok), 1)
             <= lax.broadcasted_iota(jnp.int32, (tok, tok), 0))

    def transposed(a, b):
        return lax.dot_general(a, b, (((1,), (1,)), ((), ())), precision=HIGH,
                               preferred_element_type=jnp.float32)

    def local_heads(start, count):
        @pl.loop(start, start + count)
        def _(h):
            qf[h] = feature_map(q_ref, h)
            scores = jnp.where(lower, transposed(qf[h], kf[h]), 0.0)
            both[h] = transposed(scores, vt[h])

    at_x0 = (x == 0).astype(jnp.float32)
    for g in range(GROUPS):
        part = pl.ds(g * per, per)
        hop = remote(back.at[part], below.at[part], z_send.at[g], z_recv.at[g], (up, y))

        @pl.when(has_down)
        def _():
            hop.wait_recv()

        @pl.when(z == 0)
        def _():
            below[part] = jnp.zeros((per, ROWS, M), jnp.float32)

        chip = state[pl.ds(mine + g * per, per)] + sib_state[part]
        back[part] = below[part] + chip
        xsend[part] = (below[part] + at_x0 * chip).astype(xsend.dtype)
        go(has_up, hop)
        go(None, remote(xsend.at[part], xrecv.at[part], x_send.at[g], x_recv.at[g], (xn, y)))
        local_heads(g * (heads // GROUPS), heads // GROUPS)
        if g == 1:
            along(1)

    along(2)
    across(0)
    across(1)
    at_c0, at_c1 = (c == 0).astype(jnp.float32), (c == 1).astype(jnp.float32)
    for g in range(GROUPS):
        part = pl.ds(g * per, per)
        own = pl.ds(mine + g * per, per)
        remote(xsend.at[part], xrecv.at[part], x_send.at[g], x_recv.at[g], (xn, y)).wait_recv()
        base = below[part] + xrecv[part].astype(jnp.float32)
        below[part] = base + at_c0 * state[own]
        prior[own] = base + at_c1 * sib_state[part]
        go(None, remote(below.at[part], prior.at[own], b_send.at[g], b_recv.at[g], (sib, y)))

    def finish(start):
        @pl.loop(0, half_heads)
        def _(i):
            h = start + i
            total = both[h] + transposed(qf[h], prior[h])
            att[:, head_cols(h)] = (total[:, :DH] / total[:, DH : DH + 1]).astype(att.dtype)

    finish(mine)
    along(3)
    for g in range(GROUPS):
        theirs = pl.ds(other + g * per, per)
        remote(below.at[pl.ds(g * per, per)], prior.at[theirs], b_send.at[g], b_recv.at[g],
               (sib, y)).wait_recv()
    finish(other)
    across(2)

    width = wbuf.shape[2]
    halfn = n // 2

    def out_copy(b):
        i = b % halfn
        return remote(psend.at[i], precv.at[i], p_send.at[i], p_recv.at[i], (me, 1 - y))

    def bit(a, b):
        return (a + b) % 2

    def project(first, count):
        @pl.loop(first, first + count)
        def _(i):
            b = ((bit(z // 2, i // 8) * 2 + bit(z % 2, (i // 4) % 2)) * PLANE
                 + bit(x, (i // 2) % 2) * 2 + bit(c, i % 2))

            @pl.when(i % 2 == 1)
            def _():
                arrived(b)
            piece = jnp.dot(att[...], wbuf[b], preferred_element_type=jnp.float32)

            @pl.when(b // halfn == y)
            def _():
                acc[b % halfn] = piece

            @pl.when(b // halfn != y)
            def _():
                psend[b % halfn] = piece.astype(psend.dtype)
                out_copy(b).start()

    project(0, 3 * PLANE)
    across(3)
    project(3 * PLANE, PLANE)
    for i in range(halfn):
        out_copy(i).wait_recv()
        out_ref[:, i * width : (i + 1) * width] = (
            acc[i] + precv[i].astype(jnp.float32)).astype(out_ref.dtype)
    for i in range(halfn):
        out_copy(i).wait_send()
    for cond, copy in started:
        if cond is None:
            copy.wait_send()
        else:
            pl.when(cond)(copy.wait_send)


def fused(queries, keys, values, features, weight):
    tok, columns = queries.shape
    heads = features.shape[0]
    n = lax.axis_size("seq")
    depth, width = weight.shape
    half = heads // 2
    f32, bf16 = jnp.float32, jnp.bfloat16
    vmem = pltpu.VMEM
    dma = pltpu.SemaphoreType.DMA
    inner = [pl.BlockSpec(memory_space=pltpu.VMEM)] * 4
    return pl.pallas_call(
        functools.partial(kernel_body, heads),
        out_shape=jax.ShapeDtypeStruct((tok, width * n // 2), bf16),
        in_specs=inner + [pl.BlockSpec(memory_space=pl.ANY)],
        out_specs=pl.BlockSpec(memory_space=pltpu.VMEM),
        scratch_shapes=[
            vmem((n, depth, width), bf16),
            vmem((heads, tok, M), f32),
            vmem((heads, tok, M), f32),
            vmem((heads, ROWS, tok), f32),
            vmem((heads, tok, ROWS), f32),
            vmem((heads, ROWS, M), f32),
            vmem((half, ROWS, M), f32),
            vmem((half, ROWS, M), f32),
            vmem((half, ROWS, M), bf16),
            vmem((half, ROWS, M), bf16),
            vmem((heads, ROWS, M), f32),
            vmem((half, ROWS, M), f32),
            vmem((tok, columns), bf16),
            vmem((n // 2, tok, width), f32),
            vmem((n // 2, tok, width), bf16),
            vmem((n // 2, tok, width), bf16),
            dma, dma((n, 4)), dma((n,)), dma, dma,
            dma((GROUPS,)), dma((GROUPS,)), dma((GROUPS,)), dma((GROUPS,)),
            dma((GROUPS,)), dma((GROUPS,)), dma((n // 2,)), dma((n // 2,)),
        ],
        compiler_params=pltpu.CompilerParams(
            collective_id=0, has_side_effects=True, vmem_limit_bytes=63 << 20),
    )(queries, keys, values, features, weight)


def shards(queries, keys, values, features, output_proj_weight):
    fits = (
        lax.axis_size("seq") == PLANE * DEPTH
        and lax.axis_size("head") == 2
        and features.shape[0] % (2 * GROUPS) == 0
        and output_proj_weight.shape[1] % 128 == 0
    )
    step = fused if fits else plain
    return step(queries, keys, values, features, output_proj_weight)


def solution(mesh):
    in_specs = (
        P("seq", "head"),
        P("seq", "head"),
        P("seq", "head"),
        P("head", None, None),
        P("head", "seq"),
    )
    return jax.shard_map(
        shards, mesh=mesh, in_specs=in_specs, out_specs=P("seq", "head"), check_vma=False
    )
```
